512 devices in a mesh: dp: 64 (over z, x, core), expert: 8 (over y).
Axes of the slice: x: 4, y: 8, z: 8, core: 2. Of those that a mesh axis runs over, the one named last changes fastest.
Arguments:
- tokens: bfloat16 [512, 4096], P('expert', 'dp'), may hold values from -6 to 6
- cotangent: bfloat16 [512, 4096], P('expert', 'dp'), may hold values from -6 to 6
- gate_logit: float32 [512], P('expert'), may hold values from -8 to 8
- routes: int32 [512, 2], P('expert'), may hold values from 0 to 7, all different within a row; in each aligned block of 64 rows (0 to 63, 64 to 127, ...) at most 32 rows name the same one
- w_up: bfloat16 [8, 14336, 4096], P('expert', 'dp'), may hold values from -0.09375 to 0.09375
- w_down: bfloat16 [8, 14336, 4096], P('expert', 'dp'), may hold values from -0.046875 to 0.046875
- basis: bfloat16 [4096, 256], P('dp'), may hold values from -0.09375 to 0.09375
- sketch: float32 [8, 256, 256], P('expert'), may hold values from -1 to 10, as said below
Outputs:
- token_grad: bfloat16 [512, 4096], P('expert', 'dp')
- sketch_next: float32 [8, 256, 256], P('expert')
- precond: float32 [8, 14336, 256], P('expert', 'dp')
The draws below stay inside these ranges and needn't reach their ends.
Inputs may be any that keep to these rules, and one draw needn't show every extreme that they name: `routes`: each row names 2 different experts. Among the 64 tokens of one index of expert at most 32 name the same expert, and in some index that many do. `sketch`: each matrix is symmetric, and in every row its diagonal entry exceeds the sum of the magnitudes off the diagonal.
All inputs are finite; a program needn't handle non-finite values.
Results may differ from the reference program's by a relative error of at most 0.0064.
Values may be sent and summed in bfloat16 or wider, within the bound.
A program may use at most 128 MiB of HBM per device.

```python
import math
import jax
import jax.numpy as jnp
import numpy as np
from jax import lax

D = 4096
FF = 14336
TOP = 2
RANK = 256
TOK_SH = 64
EXPERTS = 8
CAP = 32
TOKENS = 512
N_EXPERT = 8


def draw_sketch(key, part):
    key_diag, key_off = jax.random.split(jax.random.fold_in(key, 7))
    diag_vals = jnp.exp(jax.random.uniform(key_diag, (EXPERTS, RANK), jnp.float32, 0.0, math.log(10.0)))
    raw_vals = jnp.clip(jax.random.normal(key_off, (EXPERTS, RANK, RANK), jnp.float32), -1.0, 1.0)
    symmetric = (raw_vals + jnp.swapaxes(raw_vals, 1, 2)) * (0.5 / RANK)
    identity = jnp.eye(RANK, dtype=jnp.float32)
    return symmetric * (1.0 - identity) + diag_vals[:, :, None] * identity


def level_of(stream_key, dims, shards, smallest, largest):
    factor_of = 1.0
    for dim, blocks in shards:
        heights = jax.random.uniform(jax.random.fold_in(jax.random.fold_in(stream_key, 6), dim), (blocks,), jnp.float32, smallest / len(shards), largest / len(shards))
        factor_of = factor_of * jnp.repeat(jnp.exp(heights), dims[dim] // blocks).reshape((-1,) + (1,) * (len(dims) - 1 - dim))
    return factor_of


def shared_out(rng, own, number, rows, number_of, top, reach, skew):
    order = jax.random.permutation(rng, number_of)
    heavy_load, common = shares(number_of, rows * top, reach, skew, True), shares(number_of, rows * top, reach, skew, False)
    places = jnp.arange(number_of)

    def named(lengths, turn):
        used = int((lengths > 0).sum())
        fixed = max(1, used // 4)
        passed = fixed + (places - fixed + turn * (used - fixed)) % max(1, number_of - fixed)
        return jnp.zeros((number_of,), jnp.int32).at[order[jnp.where(places < fixed, places, passed)]].set(jnp.asarray(lengths, jnp.int32))

    lengths = jnp.where(number % 4 == 0, named(heavy_load, number // 4), named(common, number - number // 4 - 1))
    mixed = jax.random.permutation(jax.random.fold_in(own, 3), number_of)
    donor, taker = mixed[0:number_of // 2 * 2:2], mixed[1:number_of // 2 * 2:2]
    slack = jnp.minimum(lengths[donor] - 1, reach - lengths[taker]) // 2
    slack = jnp.where((donor == order[0]) | (taker == order[0]) | (lengths[taker] == 0), 0, jnp.maximum(slack, 0))
    passed = jax.random.randint(jax.random.fold_in(own, 4), (number_of // 2,), 0, 1 << 20) % (slack + 1)
    lengths = lengths.at[donor].add(-passed).at[taker].add(passed)
    labels = jnp.searchsorted(jnp.cumsum(lengths), jnp.arange(rows * top), side="right").astype(jnp.int32)
    table = labels.reshape(top, rows).T
    table = table[jax.random.permutation(jax.random.fold_in(own, 1), rows)]
    turn = jax.random.randint(jax.random.fold_in(own, 2), (rows, 1), 0, top)
    return jnp.take_along_axis(table, (jnp.arange(top)[None, :] + turn) % top, axis=1)


def shares(count, total, limit, slope, full):
    weights = [(1 << 20) // math.isqrt(rank ** slope) + 1 for rank in range(1, count + 1)]
    largest = limit if full else min(limit, max(-(-total // count), total * weights[0] // sum(weights)))
    least = 1 if total - largest >= count - 1 else 0
    counts, spare = [largest] + [least] * (count - 1), total - largest - least * (count - 1)
    while spare > 0:
        free = [i for i in range(1, count) if counts[i] < largest] or [i for i in range(1, count) if counts[i] < limit]
        pool, budget = sum([weights[i] for i in free]), spare
        for i in free:
            addition = min(limit - counts[i], max(1, budget * weights[i] // pool), spare)
            counts[i] = counts[i] + addition
            spare = spare - addition
    return np.array(counts)


def noise(rng, extent, deviation, most, cuts=(), kind=jnp.bfloat16):
    values = jax.random.normal(rng, extent, jnp.float32) * deviation
    if len(cuts) > 0:
        values = level_of(rng, extent, cuts, -0.22, 0.18) * values
    return jnp.clip(values, min=-most, max=most).astype(kind)


def setup_inputs(seed: int = 0) -> dict:
    splits = jax.random.split(jax.random.key(seed), 9)
    tokens = noise(splits[0], (TOKENS, D), 1.0, 6.0, ((0, 8), (1, 64)))
    cotangent = noise(splits[1], (TOKENS, D), 1.0, 6.0, ((0, 8), (1, 64)))
    gate_logit = noise(splits[2], (TOKENS,), 2.0, 8.0, ((0, 8),), jnp.float32)
    routes_keys = jax.random.split(jax.random.fold_in(splits[3], 1), TOKENS // TOK_SH)
    routes_turns = jax.random.permutation(jax.random.fold_in(splits[3], 3), TOKENS // TOK_SH)
    routes = jax.vmap(lambda own, number: shared_out(jax.random.fold_in(splits[3], 2), own, number, TOK_SH, EXPERTS, TOP, CAP, 2))(routes_keys, routes_turns).reshape((TOKENS, TOP))
    w_up = noise(splits[4], (EXPERTS, FF, D), D ** -0.5, 0.09375, ((0, 8), (1, 64)))
    w_down = noise(splits[5], (EXPERTS, FF, D), FF ** -0.5, 0.046875, ((0, 8), (1, 64)))
    basis = noise(splits[6], (D, RANK), D ** -0.5, 0.09375, ((0, 64),))
    sketch = draw_sketch(jax.random.fold_in(splits[8], 71), 0)
    return {"tokens": tokens, "cotangent": cotangent, "gate_logit": gate_logit, "routes": routes, "w_up": w_up, "w_down": w_down, "basis": basis, "sketch": sketch}


decay_rate = 0.9
damping = 1.0
highest = lax.Precision.HIGHEST

def rounded(value):
    return lax.optimization_barrier(value.astype(jnp.bfloat16)).astype(jnp.float32)

def slot_table(routes):
    expert_ids = jnp.arange(EXPERTS, dtype=jnp.int32)
    hit_count = jnp.sum((routes[:, :, None] == expert_ids[None, None, :]).astype(jnp.int32), axis=1)
    blocks = hit_count.reshape(TOKENS // TOK_SH, TOK_SH, EXPERTS)
    before = (jnp.cumsum(blocks, axis=1) - blocks).reshape(TOKENS, EXPERTS)
    source = jnp.arange(TOKENS, dtype=jnp.int32) // TOK_SH
    slot_index = source[:, None] * CAP + before
    return (hit_count, slot_index)

def reference(tokens, cotangent, gate_logit, routes, w_up, w_down, basis, sketch):
    gate_first = jax.nn.sigmoid(gate_logit.astype(jnp.float32))
    gates = jnp.stack([gate_first, 1.0 - gate_first], axis=1)
    expert_ids = jnp.arange(EXPERTS, dtype=jnp.int32)
    chosen = (routes[:, :, None] == expert_ids[None, None, :]).astype(jnp.float32)
    gate_by_expert = jnp.sum(chosen * gates[:, :, None], axis=1)
    hit_count, slot_index = slot_table(routes)
    slot_ids = jnp.arange(N_EXPERT * CAP, dtype=jnp.int32)
    tok_f = tokens.astype(jnp.float32)
    cot_f = cotangent.astype(jnp.float32)
    basis_f = basis.astype(jnp.float32)
    grad_sum = jnp.zeros((TOKENS, D), jnp.float32)
    sketches = []
    precs = []
    for expert in range(EXPERTS):
        table = ((slot_index[:, expert][None, :] == slot_ids[:, None]) & (hit_count[:, expert][None, :] > 0)).astype(jnp.float32)
        x_rows = jnp.dot(table, tok_f, precision=highest)
        dy_rows = rounded(jnp.dot(table, cot_f * gate_by_expert[:, expert:expert + 1], precision=highest))
        up_f = w_up[expert].astype(jnp.float32)
        down_f = w_down[expert].astype(jnp.float32)
        hidden = jnp.dot(x_rows, up_f.T, precision=highest)
        back_grad = jnp.dot(dy_rows, down_f.T, precision=highest)
        sigma_val = jax.nn.sigmoid(hidden)
        hidden_grad = rounded(back_grad * sigma_val * (1.0 + hidden * (1.0 - sigma_val)))
        row_grad = rounded(jnp.dot(hidden_grad, up_f, precision=highest))
        grad_sum = grad_sum + jnp.dot(table.T, row_grad, precision=highest)
        projected = rounded(jnp.dot(x_rows, basis_f, precision=highest))
        coefficients = jnp.dot(projected.T, hidden_grad, precision=highest)
        gram_total = jnp.dot(coefficients, coefficients.T, precision=highest) / FF
        merged = decay_rate * sketch[expert] + gram_total
        factor = jnp.linalg.cholesky(merged + damping * jnp.eye(RANK, dtype=jnp.float32))
        solved = damping * jax.scipy.linalg.cho_solve((factor, True), coefficients)
        sketches.append(merged)
        precs.append(solved.T)
    return (grad_sum.astype(jnp.bfloat16), jnp.stack(sketches), jnp.stack(precs))
```

```python
import functools

import jax
import jax.numpy as jnp
from jax import lax
from jax.experimental import pallas as pl
from jax.experimental.pallas import tpu as pltpu
from jax.sharding import PartitionSpec as P

decay_rate = 0.9
damping = 1.0
highest = lax.Precision.HIGHEST
MESH = pl.DeviceIdType.MESH
CORES = 2
WIDE = 4
bf16 = jnp.bfloat16
f32 = jnp.float32
VMEM = pl.BlockSpec(memory_space=pltpu.VMEM)
ANY = pl.BlockSpec(memory_space=pl.ANY)


def greet(axis, peers):
    barrier = pltpu.get_barrier_semaphore()
    for peer in peers:
        pl.semaphore_signal(barrier, inc=1, device_id={axis: peer}, device_id_type=MESH)
    pl.semaphore_wait(barrier, len(peers))


def remote(src, dst, send, recv, axis, peer):
    copy = pltpu.make_async_remote_copy(
        src_ref=src,
        dst_ref=dst,
        send_sem=send,
        recv_sem=recv,
        device_id={axis: peer},
        device_id_type=MESH,
    )
    copy.start()
    return copy


def exchange_kernel(n, src, dst, send, recv, own):
    me = lax.axis_index("expert")
    peers = [lax.rem(me + k, n) for k in range(1, n)]
    greet("expert", peers)
    copies = [
        remote(src.at[peer], dst.at[me], send.at[k], recv.at[k], "expert", peer)
        for k, peer in enumerate(peers)
    ]
    mine = pltpu.make_async_copy(src.at[me], dst.at[me], own)
    mine.start()
    for copy in copies:
        copy.wait()
    mine.wait()


def exchange(value, n, number):
    return pl.pallas_call(
        functools.partial(exchange_kernel, n),
        out_shape=jax.ShapeDtypeStruct(value.shape, value.dtype),
        in_specs=[VMEM],
        out_specs=VMEM,
        scratch_shapes=[
            pltpu.SemaphoreType.DMA((n,)),
            pltpu.SemaphoreType.DMA((n,)),
            pltpu.SemaphoreType.DMA,
        ],
        compiler_params=pltpu.CompilerParams(collective_id=number, has_side_effects=True),
    )(value)


def place(deep):
    me = lax.axis_index("dp")
    core = lax.rem(me, CORES)
    chip = me // CORES
    return chip // WIDE, lax.rem(chip, WIDE), core


def index_of(z, x, core):
    return (z * WIDE + x) * CORES + core


def gather_kernel(
    deep, x_in, dy_in, basis_in, up_hbm, down_hbm, r_out, c_out, gram_out,
    xs, dys, bases, up, down, hid, back, proj, sent, got, ring_send, ring_recv, share_send, share_recv,
):
    z, x, core = place(deep)
    other = 1 - core
    partner = index_of(z, x, other)
    sizes = {"z": deep, "x": WIDE}
    spot = {"z": z, "x": x}

    def near(axis, step):
        at = lax.rem(spot[axis] + step + sizes[axis], sizes[axis])
        return index_of(at, x, core) if axis == "z" else index_of(z, at, core)

    fetch_up = pltpu.make_async_copy(up_hbm, up, got.at[0])
    fetch_down = pltpu.make_async_copy(down_hbm, down, got.at[1])
    fetch_up.start()
    fetch_down.start()
    greet("dp", [near("z", 1), near("z", -1), near("x", 1), near("x", -1), partner])

    full = [xs, dys, bases]
    starts = [x_in, dy_in, basis_in]
    orders = [("z", "x"), ("x", "z"), ("z", "x")]
    own = []
    for t in range(3):
        copy = pltpu.make_async_copy(starts[t], full[t].at[z, x, core], sent.at[t])
        copy.start()
        own.append(copy)
    sends = []
    flows = []

    def block(t, axis, at, half=None):
        rows = slice(None) if half is None else pl.ds(half * 32, 32)
        return full[t].at[at, x, core, rows] if axis == "z" else full[t].at[z, at, core, rows]

    def slab(t, axis, at, half=None):
        if axis == "x":
            part = slice(None) if half is None else pl.ds(half * (deep // 2), deep // 2)
            return full[t].at[part, at, core]
        part = slice(None) if half is None else pl.ds(half * (WIDE // 2), WIDE // 2)
        return full[t].at[at, part, core]

    def ring_step(t, phase, axis, step, view):
        last = sizes[axis] // 2
        copies = []
        for way, sign in enumerate((1, -1)):
            at = lax.rem(spot[axis] - sign * (step - 1) + sizes[axis], sizes[axis])
            piece = view(t, axis, at, way if step == last else None)
            source = piece
            if phase == 0 and step == 1:
                source = starts[t] if step != last else starts[t].at[pl.ds(way * 32, 32)]
            copies.append(
                remote(
                    source, piece, ring_send.at[t, phase, way, step - 1],
                    ring_recv.at[t, phase, way, step - 1], "dp", near(axis, sign),
                )
            )
        sends.extend(copies)
        return copies

    shares = []

    def share(t, axis, at):
        piece = slab(t, axis, at)
        number = 0
        for old in shares:
            number += old[0] == t
        copy = remote(
            piece, piece, share_send.at[t, number], share_recv.at[t, number], "dp", partner
        )
        shares.append((t, copy))

    def stages(t):
        first, second = orders[t]
        for step in range(1, sizes[first] // 2 + 1):
            copies = ring_step(t, 0, first, step, block)
            yield
            for copy in copies:
                copy.wait_recv()
        own[t].wait()
        at = spot[second]
        n = sizes[second]
        copies = ring_step(t, 1, second, 1, slab)
        share(t, second, at)
        yield
        for step in range(1, n // 2):
            for copy in copies:
                copy.wait_recv()
            copies = ring_step(t, 1, second, step + 1, slab)
            share(t, second, lax.rem(at - step + n, n))
            share(t, second, lax.rem(at + step, n))
            yield
        for copy in copies:
            copy.wait_recv()
        share(t, second, lax.rem(at + n // 2, n))

    flows = [stages(t) for t in range(3)]
    while flows:
        for flow in list(flows):
            if next(flow, flow) is flow:
                flows.remove(flow)
    fetch_up.wait()
    fetch_down.wait()
    for copy in sends:
        copy.wait_send()
    for _, copy in shares:
        copy.wait()

    chunk = WIDE * CORES * 64
    hid[...] = jnp.zeros_like(hid)
    back[...] = jnp.zeros_like(back)
    proj[...] = jnp.zeros_like(proj)
    turned = (((0,), (0,)), ((), ()))

    def forward(at, carry):
        columns = pl.ds(pl.multiple_of(at * chunk, chunk), chunk)
        x_part = xs[at].reshape(chunk, 256)
        dy_part = dys[at].reshape(chunk, 256)
        basis_part = bases[at].reshape(chunk, 256)
        hid[...] += jnp.dot(up[:, columns], x_part, preferred_element_type=f32)
        back[...] += jnp.dot(down[:, columns], dy_part, preferred_element_type=f32)
        proj[...] += lax.dot_general(x_part, basis_part, turned, preferred_element_type=f32)
        return carry

    lax.fori_loop(0, deep, forward, 0)
    hidden = hid[...]
    sigma = jax.nn.sigmoid(hidden)
    grad = (back[...] * sigma * (1.0 + hidden * (1.0 - sigma))).astype(bf16)
    coef = jnp.dot(grad, proj[...].astype(bf16), preferred_element_type=f32)
    c_out[...] = coef
    gram_out[...] = lax.dot_general(
        coef, coef, turned, precision=highest, preferred_element_type=f32
    )

    def rows(at, carry):
        columns = pl.ds(pl.multiple_of(at * chunk, chunk), chunk)
        part = lax.dot_general(up[:, columns], grad, turned, preferred_element_type=f32)
        r_out[at] = part.astype(bf16).reshape(WIDE, CORES, 64, 256)
        return carry

    lax.fori_loop(0, deep, rows, 0)


def gather_compute(x_t, dy_t, basis, up, down, deep):
    units, width = up.shape
    blocks = (deep, WIDE, CORES, 64, 256)
    steps = max(deep, WIDE)
    return pl.pallas_call(
        functools.partial(gather_kernel, deep),
        out_shape=(
            jax.ShapeDtypeStruct(blocks, bf16),
            jax.ShapeDtypeStruct((units, 256), f32),
            jax.ShapeDtypeStruct((256, 256), f32),
        ),
        in_specs=[VMEM, VMEM, VMEM, ANY, ANY],
        out_specs=(VMEM, VMEM, VMEM),
        scratch_shapes=[
            pltpu.VMEM(blocks, bf16),
            pltpu.VMEM(blocks, bf16),
            pltpu.VMEM(blocks, bf16),
            pltpu.VMEM((units, width), bf16),
            pltpu.VMEM((units, width), bf16),
            pltpu.VMEM((units, 256), f32),
            pltpu.VMEM((units, 256), f32),
            pltpu.VMEM((256, 256), f32),
            pltpu.SemaphoreType.DMA((3,)),
            pltpu.SemaphoreType.DMA((2,)),
            pltpu.SemaphoreType.DMA((3, 2, 2, steps // 2)),
            pltpu.SemaphoreType.DMA((3, 2, 2, steps // 2)),
            pltpu.SemaphoreType.DMA((3, steps)),
            pltpu.SemaphoreType.DMA((3, steps)),
        ],
        compiler_params=pltpu.CompilerParams(
            collective_id=1, has_side_effects=True, vmem_limit_bytes=40 << 20
        ),
    )(x_t, dy_t, basis, up, down)


def reduce_kernel(
    deep, r_in, gram_in, r_out, gram_out,
    g0, gsum, gx, gz, r0, rsum, rx, r1, rz, core_send, core_recv, x_send, x_recv, z_send, z_recv,
):
    z, x, core = place(deep)
    other = 1 - core
    partner = index_of(z, x, other)
    x_at = [lax.rem(x + k, WIDE) for k in range(1, WIDE)]
    z_at = [lax.rem(z + k, deep) for k in range(1, deep)]
    x_peers = [index_of(z, at, core) for at in x_at]
    z_peers = [index_of(at, x, core) for at in z_at]
    greet("dp", [partner] + x_peers + z_peers)

    def to_core(number, src, dst):
        return remote(src, dst, core_send.at[number], core_recv.at[number], "dp", partner)

    def along_x(number, pairs):
        return [
            remote(src, dst, x_send.at[number, k], x_recv.at[number, k], "dp", x_peers[k])
            for k, (src, dst) in enumerate(pairs)
        ]

    def along_z(number, pairs):
        return [
            remote(src, dst, z_send.at[number, k], z_recv.at[number, k], "dp", z_peers[k])
            for k, (src, dst) in enumerate(pairs)
        ]

    gram_core = to_core(0, gram_in.at[other], g0)
    r_core = to_core(1, r_in.at[:, :, other], r0)

    gram_core.wait_recv()
    gsum[...] = gram_in[core] + g0[...]
    gram_x = along_x(0, [(gsum.at[at], gx.at[x]) for at in x_at])

    r_core.wait_recv()

    def add_core(at, carry):
        rsum[at] = (r_in[at, :, core].astype(f32) + r0[at].astype(f32)).astype(bf16)
        return carry

    lax.fori_loop(0, deep, add_core, 0)

    for copy in gram_x:
        copy.wait_recv()
    total = gsum[x]
    for at in x_at:
        total = total + gx[at]
    gz[z] = total
    gram_z = along_z(0, [(gz.at[z], gz.at[z]) for _ in z_at])
    r_x = along_x(1, [(rsum.at[:, at], rx.at[x]) for at in x_at])

    for copy in gram_z:
        copy.wait_recv()
    total = gz[0]
    for at in range(1, deep):
        total = total + gz[at]
    gram_out[core, x] = total
    gram_back = along_x(2, [(gram_out.at[core, x], gram_out.at[core, x]) for _ in x_at])

    for copy in r_x:
        copy.wait_recv()

    def add_x(at, carry):
        part = rsum[at, x].astype(f32)
        for peer in x_at:
            part = part + rx[peer, at].astype(f32)
        r1[at] = part.astype(bf16)
        return carry

    lax.fori_loop(0, deep, add_x, 0)
    r_z = along_z(1, [(r1.at[at], rz.at[z]) for at in z_at])
    for copy in gram_back:
        copy.wait_recv()
    gram_last = to_core(2, gram_out.at[core], gram_out.at[core])
    for copy in r_z:
        copy.wait_recv()
    part = r1[z].astype(f32)
    for at in z_at:
        part = part + rz[at].astype(f32)
    r_out[...] = part.astype(bf16)
    gram_last.wait_recv()
    for copy in [gram_core, r_core, gram_last] + gram_x + r_x + gram_back + gram_z + r_z:
        copy.wait_send()


def reduce_all(r_part, gram_part, deep):
    rows = 256 // (CORES * WIDE)
    gram_shape = (CORES, WIDE, rows, 256)
    r_sum, gram_sum = pl.pallas_call(
        functools.partial(reduce_kernel, deep),
        out_shape=(
            jax.ShapeDtypeStruct((64, 256), bf16),
            jax.ShapeDtypeStruct(gram_shape, f32),
        ),
        in_specs=[VMEM, VMEM],
        out_specs=(VMEM, VMEM),
        scratch_shapes=[
            pltpu.VMEM((WIDE, rows, 256), f32),
            pltpu.VMEM((WIDE, rows, 256), f32),
            pltpu.VMEM((WIDE, rows, 256), f32),
            pltpu.VMEM((deep, rows, 256), f32),
            pltpu.VMEM((deep, WIDE, 64, 256), bf16),
            pltpu.VMEM((deep, WIDE, 64, 256), bf16),
            pltpu.VMEM((WIDE, deep, 64, 256), bf16),
            pltpu.VMEM((deep, 64, 256), bf16),
            pltpu.VMEM((deep, 64, 256), bf16),
            pltpu.SemaphoreType.DMA((3,)),
            pltpu.SemaphoreType.DMA((3,)),
            pltpu.SemaphoreType.DMA((3, WIDE)),
            pltpu.SemaphoreType.DMA((3, WIDE)),
            pltpu.SemaphoreType.DMA((2, deep)),
            pltpu.SemaphoreType.DMA((2, deep)),
        ],
        compiler_params=pltpu.CompilerParams(
            collective_id=2, has_side_effects=True, vmem_limit_bytes=40 << 20
        ),
    )(r_part, gram_part.reshape(gram_shape))
    return r_sum, gram_sum.reshape(256, 256)


def per_device(tokens, cotangent, gate_logit, routes, w_up, w_down, basis, sketch):
    experts = lax.axis_size("expert")
    deep = lax.axis_size("dp") // (WIDE * CORES)
    tok_rows, width_local = tokens.shape
    capacity = min(tok_rows, tok_rows * 4 // experts)
    slot_count = experts * capacity
    gate_first = jax.nn.sigmoid(gate_logit)
    gates = jnp.stack([gate_first, 1.0 - gate_first], axis=1)
    expert_ids = jnp.arange(experts, dtype=jnp.int32)
    chosen = routes[:, :, None] == expert_ids[None, None, :]
    hit_count = jnp.sum(chosen.astype(jnp.int32), axis=1)
    gate_by_expert = jnp.sum(chosen.astype(f32) * gates[:, :, None], axis=1)
    before = jnp.cumsum(hit_count, axis=0) - hit_count
    slot_of = expert_ids[None, :] * capacity + before
    slot_ids = jnp.arange(slot_count, dtype=jnp.int32)
    slot_match = (
        (slot_of[None, :, :] == slot_ids[:, None, None]) & (hit_count[None, :, :] > 0)
    ).astype(f32)
    table = jnp.sum(slot_match, axis=2)
    gate_slot = jnp.sum(slot_match * gate_by_expert[None, :, :], axis=(1, 2))
    table_b = table.astype(bf16)
    both = jnp.concatenate([tokens, cotangent], axis=1)
    picked = jnp.dot(table_b, both, preferred_element_type=f32)
    scale = jnp.where(jnp.arange(2 * width_local)[None, :] < width_local, 1.0, gate_slot[:, None])
    packed = (picked * scale).astype(bf16).reshape(experts, capacity, 2 * width_local)
    arrived = exchange(packed, experts, 0).reshape(slot_count, 2 * width_local).T
    r_part, coef_t, gram_part = gather_compute(
        arrived[:width_local], arrived[width_local:], basis, w_up[0], w_down[0], deep
    )
    r_sum, gram_total = reduce_all(r_part, gram_part, deep)
    rows = jnp.pad(r_sum.T, ((0, 0), (0, 128 - width_local)))
    returned = exchange(rows.reshape(experts, capacity, 128), experts, 3)
    token_grad = lax.dot_general(
        table_b,
        returned.reshape(slot_count, 128)[:, :width_local],
        (((0,), (0,)), ((), ())),
        preferred_element_type=f32,
    ).astype(bf16)
    total_hidden = w_up.shape[1] * lax.axis_size("dp")
    merged = decay_rate * sketch[0] + gram_total / total_hidden
    factor = jnp.linalg.cholesky(merged + damping * jnp.eye(merged.shape[0], dtype=f32))
    solved = damping * jax.scipy.linalg.cho_solve((factor, True), coef_t.T)
    return (token_grad, merged[None], solved.T[None])


def solution(mesh):
    in_specs = (
        P("expert", "dp"),
        P("expert", "dp"),
        P("expert"),
        P("expert", None),
        P("expert", "dp", None),
        P("expert", "dp", None),
        P("dp", None),
        P("expert", None, None),
    )
    out_specs = (P("expert", "dp"), P("expert", None, None), P("expert", "dp", None))
    return jax.shard_map(
        per_device, mesh=mesh, in_specs=in_specs, out_specs=out_specs, check_vma=False
    )
```

```python
import functools

import jax
import jax.numpy as jnp
from jax import lax
from jax.experimental import pallas as pl
from jax.experimental.pallas import tpu as pltpu
from jax.sharding import PartitionSpec as P

decay_rate = 0.9
damping = 1.0
highest = lax.Precision.HIGHEST
MESH = pl.DeviceIdType.MESH
CORES = 2
WIDE = 4
bf16 = jnp.bfloat16
f32 = jnp.float32
VMEM = pl.BlockSpec(memory_space=pltpu.VMEM)
ANY = pl.BlockSpec(memory_space=pl.ANY)


def greet(axis, peers):
    barrier = pltpu.get_barrier_semaphore()
    for peer in peers:
        pl.semaphore_signal(barrier, inc=1, device_id={axis: peer}, device_id_type=MESH)
    pl.semaphore_wait(barrier, len(peers))


def remote(src, dst, send, recv, axis, peer):
    copy = pltpu.make_async_remote_copy(
        src_ref=src,
        dst_ref=dst,
        send_sem=send,
        recv_sem=recv,
        device_id={axis: peer},
        device_id_type=MESH,
    )
    copy.start()
    return copy


def exchange_kernel(n, src, dst, send, recv, own):
    me = lax.axis_index("expert")
    peers = [lax.rem(me + k, n) for k in range(1, n)]
    greet("expert", peers)
    copies = [
        remote(src.at[peer], dst.at[me], send.at[k], recv.at[k], "expert", peer)
        for k, peer in enumerate(peers)
    ]
    mine = pltpu.make_async_copy(src.at[me], dst.at[me], own)
    mine.start()
    for copy in copies:
        copy.wait()
    mine.wait()


def exchange(value, n, number):
    return pl.pallas_call(
        functools.partial(exchange_kernel, n),
        out_shape=jax.ShapeDtypeStruct(value.shape, value.dtype),
        in_specs=[VMEM],
        out_specs=VMEM,
        scratch_shapes=[
            pltpu.SemaphoreType.DMA((n,)),
            pltpu.SemaphoreType.DMA((n,)),
            pltpu.SemaphoreType.DMA,
        ],
        compiler_params=pltpu.CompilerParams(collective_id=number, has_side_effects=True),
    )(value)


def place(deep):
    me = lax.axis_index("dp")
    core = lax.rem(me, CORES)
    chip = me // CORES
    return chip // WIDE, lax.rem(chip, WIDE), core


def index_of(z, x, core):
    return (z * WIDE + x) * CORES + core


def gather_kernel(
    deep, x_in, dy_in, basis_in, up_hbm, down_hbm, r_out, c_out, gram_out,
    xs, dys, bases, up, down, hid, back, proj, sent, got, ring_send, ring_recv, share_send, share_recv,
):
    z, x, core = place(deep)
    other = 1 - core
    partner = index_of(z, x, other)
    sizes = {"z": deep, "x": WIDE}
    spot = {"z": z, "x": x}

    def near(axis, step):
        at = lax.rem(spot[axis] + step + sizes[axis], sizes[axis])
        return index_of(at, x, core) if axis == "z" else index_of(z, at, core)

    fetch_up = pltpu.make_async_copy(up_hbm, up, got.at[0])
    fetch_down = pltpu.make_async_copy(down_hbm, down, got.at[1])
    fetch_up.start()
    fetch_down.start()
    greet("dp", [near("z", 1), near("z", -1), near("x", 1), near("x", -1), partner])

    full = [xs, dys, bases]
    starts = [x_in, dy_in, basis_in]
    orders = [("z", "x"), ("x", "z"), ("z", "x")]
    own = []
    for t in range(3):
        copy = pltpu.make_async_copy(starts[t], full[t].at[z, x, core], sent.at[t])
        copy.start()
        own.append(copy)
    sends = []
    flows = []

    def block(t, axis, at, half=None):
        rows = slice(None) if half is None else pl.ds(half * 32, 32)
        return full[t].at[at, x, core, rows] if axis == "z" else full[t].at[z, at, core, rows]

    def slab(t, axis, at, half=None):
        if axis == "x":
            part = slice(None) if half is None else pl.ds(half * (deep // 2), deep // 2)
            return full[t].at[part, at, core]
        part = slice(None) if half is None else pl.ds(half * (WIDE // 2), WIDE // 2)
        return full[t].at[at, part, core]

    def ring_step(t, phase, axis, step, view):
        last = sizes[axis] // 2
        copies = []
        for way, sign in enumerate((1, -1)):
            at = lax.rem(spot[axis] - sign * (step - 1) + sizes[axis], sizes[axis])
            piece = view(t, axis, at, way if step == last else None)
            source = piece
            if phase == 0 and step == 1:
                source = starts[t] if step != last else starts[t].at[pl.ds(way * 32, 32)]
            copies.append(
                remote(
                    source, piece, ring_send.at[t, phase, way, step - 1],
                    ring_recv.at[t, phase, way, step - 1], "dp", near(axis, sign),
                )
            )
        sends.extend(copies)
        return copies

    shares = []

    def share(t, axis, at):
        piece = slab(t, axis, at)
        number = 0
        for old in shares:
            number += old[0] == t
        copy = remote(
            piece, piece, share_send.at[t, number], share_recv.at[t, number], "dp", partner
        )
        shares.append((t, copy))

    def stages(t):
        first, second = orders[t]
        for step in range(1, sizes[first] // 2 + 1):
            copies = ring_step(t, 0, first, step, block)
            yield
            for copy in copies:
                copy.wait_recv()
        own[t].wait()
        at = spot[second]
        n = sizes[second]
        copies = ring_step(t, 1, second, 1, slab)
        share(t, second, at)
        yield
        for step in range(1, n // 2):
            for copy in copies:
                copy.wait_recv()
            copies = ring_step(t, 1, second, step + 1, slab)
            share(t, second, lax.rem(at - step + n, n))
            share(t, second, lax.rem(at + step, n))
            yield
        for copy in copies:
            copy.wait_recv()
        share(t, second, lax.rem(at + n // 2, n))

    flows = [stages(t) for t in range(3)]
    while flows:
        for flow in list(flows):
            if next(flow, flow) is flow:
                flows.remove(flow)
    fetch_up.wait()
    fetch_down.wait()
    for copy in sends:
        copy.wait_send()
    for _, copy in shares:
        copy.wait()

    chunk = WIDE * CORES * 64
    hid[...] = jnp.zeros_like(hid)
    back[...] = jnp.zeros_like(back)
    proj[...] = jnp.zeros_like(proj)
    turned = (((0,), (0,)), ((), ()))

    def forward(at, carry):
        columns = pl.ds(pl.multiple_of(at * chunk, chunk), chunk)
        x_part = xs[at].reshape(chunk, 256)
        dy_part = dys[at].reshape(chunk, 256)
        basis_part = bases[at].reshape(chunk, 256)
        hid[...] += jnp.dot(up[:, columns], x_part, preferred_element_type=f32)
        back[...] += jnp.dot(down[:, columns], dy_part, preferred_element_type=f32)
        proj[...] += lax.dot_general(x_part, basis_part, turned, preferred_element_type=f32)
        return carry

    lax.fori_loop(0, deep, forward, 0)
    hidden = hid[...]
    sigma = jax.nn.sigmoid(hidden)
    grad = (back[...] * sigma * (1.0 + hidden * (1.0 - sigma))).astype(bf16)
    coef = jnp.dot(grad, proj[...].astype(bf16), preferred_element_type=f32)
    c_out[...] = coef
    gram_out[...] = lax.dot_general(
        coef, coef, turned, precision=highest, preferred_element_type=f32
    )

    def rows(at, carry):
        columns = pl.ds(pl.multiple_of(at * chunk, chunk), chunk)
        part = lax.dot_general(up[:, columns], grad, turned, preferred_element_type=f32)
        r_out[at] = part.astype(bf16).reshape(WIDE, CORES, 64, 256)
        return carry

    lax.fori_loop(0, deep, rows, 0)


def gather_compute(x_t, dy_t, basis, up, down, deep):
    units, width = up.shape
    blocks = (deep, WIDE, CORES, 64, 256)
    steps = max(deep, WIDE)
    return pl.pallas_call(
        functools.partial(gather_kernel, deep),
        out_shape=(
            jax.ShapeDtypeStruct(blocks, bf16),
            jax.ShapeDtypeStruct((units, 256), f32),
            jax.ShapeDtypeStruct((256, 256), f32),
        ),
        in_specs=[VMEM, VMEM, VMEM, ANY, ANY],
        out_specs=(VMEM, VMEM, VMEM),
        scratch_shapes=[
            pltpu.VMEM(blocks, bf16),
            pltpu.VMEM(blocks, bf16),
            pltpu.VMEM(blocks, bf16),
            pltpu.VMEM((units, width), bf16),
            pltpu.VMEM((units, width), bf16),
            pltpu.VMEM((units, 256), f32),
            pltpu.VMEM((units, 256), f32),
            pltpu.VMEM((256, 256), f32),
            pltpu.SemaphoreType.DMA((3,)),
            pltpu.SemaphoreType.DMA((2,)),
            pltpu.SemaphoreType.DMA((3, 2, 2, steps // 2)),
            pltpu.SemaphoreType.DMA((3, 2, 2, steps // 2)),
            pltpu.SemaphoreType.DMA((3, steps)),
            pltpu.SemaphoreType.DMA((3, steps)),
        ],
        compiler_params=pltpu.CompilerParams(
            collective_id=1, has_side_effects=True, vmem_limit_bytes=60 << 20
        ),
    )(x_t, dy_t, basis, up, down)


def invert(matrix):
    n, group = 128, 16
    lane = lax.broadcasted_iota(jnp.int32, (1, n), 1)
    row = lax.broadcasted_iota(jnp.int32, (group, n), 0)

    def pivots(_, parts):
        top, rest = parts
        for k in range(0, group, 2):
            first = jnp.broadcast_to(top[:, k : k + 1], (group, n))
            second = jnp.broadcast_to(top[:, k + 1 : k + 2], (group, n))
            first_rest = jnp.broadcast_to(rest[:, k : k + 1], (n - group, n))
            second_rest = jnp.broadcast_to(rest[:, k + 1 : k + 2], (n - group, n))
            a, b, d = first[k : k + 1], first[k + 1 : k + 2], second[k + 1 : k + 2]
            a_inv = 1.0 / a
            slope = b * a_inv
            d_inv = 1.0 / (d - b * slope)
            p12 = -slope * d_inv
            p11 = a_inv - slope * p12
            at_first, at_second = lane == k, lane == k + 1
            row_a, row_b = top[k : k + 1], top[k + 1 : k + 2]
            u_a = p11 * row_a + p12 * row_b
            u_b = p12 * row_a + d_inv * row_b
            u_a = jnp.where(at_first, p11, jnp.where(at_second, p12, u_a))
            u_b = jnp.where(at_first, p12, jnp.where(at_second, d_inv, u_b))
            inside = at_first | at_second
            rest = jnp.where(inside, 0.0, rest) - first_rest * u_a - second_rest * u_b
            top = jnp.where(inside, 0.0, top) - first * u_a - second * u_b
            top = jnp.where(row == k, u_a, jnp.where(row == k + 1, u_b, top))
        turned = pltpu.roll(jnp.concatenate([rest, top], axis=0), n - group, 1)
        return turned[:group], turned[group:]

    top, rest = lax.fori_loop(0, n // group, pivots, (matrix[:group], matrix[group:]))
    return jnp.concatenate([top, rest], axis=0)


def exact(left, right, dims=(((1,), (0,)), ((), ()))):
    return lax.dot_general(left, right, dims, precision=highest, preferred_element_type=f32)


def reduce_kernel(
    deep, experts, hidden_total, r_in, gram_in, sketch_in, coef_in, back_out, merged_out, solved_out,
    g0, gsum, gx, gz, gram_out, r0, rsum, rx, r1, rz, ready,
    core_send, core_recv, x_send, x_recv, z_send, z_recv, y_send, y_recv, y_own,
):
    z, x, core = place(deep)
    me_y = lax.axis_index("expert")
    other = 1 - core
    partner = index_of(z, x, other)
    x_at = [lax.rem(x + k, WIDE) for k in range(1, WIDE)]
    z_at = [lax.rem(z + k, deep) for k in range(1, deep)]
    y_at = [lax.rem(me_y + k, experts) for k in range(1, experts)]
    x_peers = [index_of(z, at, core) for at in x_at]
    z_peers = [index_of(at, x, core) for at in z_at]
    barrier = pltpu.get_barrier_semaphore()
    for peer in y_at:
        pl.semaphore_signal(barrier, inc=1, device_id={"expert": peer}, device_id_type=MESH)
    for peer in [partner] + x_peers + z_peers:
        pl.semaphore_signal(barrier, inc=1, device_id={"dp": peer}, device_id_type=MESH)
    pl.semaphore_wait(barrier, 1 + len(x_peers) + len(z_peers) + len(y_at))

    def to_core(number, src, dst):
        return remote(src, dst, core_send.at[number], core_recv.at[number], "dp", partner)

    def along_x(number, pairs):
        return [
            remote(src, dst, x_send.at[number, k], x_recv.at[number, k], "dp", x_peers[k])
            for k, (src, dst) in enumerate(pairs)
        ]

    def along_z(number, pairs):
        return [
            remote(src, dst, z_send.at[number, k], z_recv.at[number, k], "dp", z_peers[k])
            for k, (src, dst) in enumerate(pairs)
        ]

    gram_core = to_core(0, gram_in.at[other], g0)
    r_core = to_core(1, r_in.at[:, :, other], r0)

    gram_core.wait_recv()
    gsum[...] = gram_in[core] + g0[...]
    gram_x = along_x(0, [(gsum.at[at], gx.at[x]) for at in x_at])

    r_core.wait_recv()

    def add_core(at, carry):
        rsum[at] = (r_in[at, :, core].astype(f32) + r0[at].astype(f32)).astype(bf16)
        return carry

    lax.fori_loop(0, deep, add_core, 0)

    for copy in gram_x:
        copy.wait_recv()
    total = gsum[x]
    for at in x_at:
        total = total + gx[at]
    gz[z] = total
    gram_z = along_z(0, [(gz.at[z], gz.at[z]) for _ in z_at])
    r_x = along_x(1, [(rsum.at[:, at], rx.at[x]) for at in x_at])

    for copy in gram_z:
        copy.wait_recv()
    total = gz[0]
    for at in range(1, deep):
        total = total + gz[at]
    gram_out[core, x] = total
    gram_back = along_x(2, [(gram_out.at[core, x], gram_out.at[core, x]) for _ in x_at])
    for copy in gram_back:
        copy.wait_recv()
    gram_last = to_core(2, gram_out.at[core], gram_out.at[core])
    gram_last.wait_recv()

    merged = decay_rate * sketch_in[...] + gram_out[...].reshape(256, 256) / hidden_total
    merged_out[...] = merged
    half = 128
    eye = (
        lax.broadcasted_iota(jnp.int32, (half, half), 0)
        == lax.broadcasted_iota(jnp.int32, (half, half), 1)
    ).astype(f32) * damping
    corner = merged[:half, half:]
    upper = invert(merged[:half, :half] + eye)
    ratio = exact(upper, corner)
    lower = merged[half:, half:] + eye - exact(merged[half:, :half], ratio)

    for copy in r_x:
        copy.wait_recv()

    def add_x(at, carry):
        part = rsum[at, x].astype(f32)
        for peer in x_at:
            part = part + rx[peer, at].astype(f32)
        r1[at] = part.astype(bf16)
        return carry

    lax.fori_loop(0, deep, add_x, 0)
    r_z = along_z(1, [(r1.at[at], rz.at[z]) for at in z_at])

    left, right = coef_in[:, :half], coef_in[:, half:]
    right = right - exact(left, ratio)
    left = exact(left, upper)
    for copy in r_z:
        copy.wait_recv()
    part = r1[z].astype(f32)
    for at in z_at:
        part = part + rz[at].astype(f32)
    part = jnp.concatenate([part, jnp.zeros_like(part)], axis=0)
    ready[...] = part.T.astype(bf16).reshape(ready.shape)
    r_y = [
        remote(ready.at[at], back_out.at[me_y], y_send.at[k], y_recv.at[k], "expert", at)
        for k, at in enumerate(y_at)
    ]
    mine = pltpu.make_async_copy(ready.at[me_y], back_out.at[me_y], y_own)
    mine.start()

    right = exact(right, invert(lower))
    solved_out[:, half:] = right * damping
    left = left - exact(right, ratio, (((1,), (1,)), ((), ())))
    solved_out[:, :half] = left * damping

    for copy in r_y:
        copy.wait_recv()
    mine.wait()
    for copy in [gram_core, r_core, gram_last] + gram_x + r_x + gram_back + gram_z + r_z + r_y:
        copy.wait_send()


def reduce_all(r_part, gram_part, sketch, coef_t, deep, experts, hidden_total):
    rows = 256 // (CORES * WIDE)
    gram_shape = (CORES, WIDE, rows, 256)
    send_shape = (experts, 256 // experts, 128)
    return pl.pallas_call(
        functools.partial(reduce_kernel, deep, experts, hidden_total),
        out_shape=(
            jax.ShapeDtypeStruct(send_shape, bf16),
            jax.ShapeDtypeStruct((256, 256), f32),
            jax.ShapeDtypeStruct(coef_t.shape, f32),
        ),
        in_specs=[VMEM] * 4,
        out_specs=(VMEM,) * 3,
        scratch_shapes=[
            pltpu.VMEM((WIDE, rows, 256), f32),
            pltpu.VMEM((WIDE, rows, 256), f32),
            pltpu.VMEM((WIDE, rows, 256), f32),
            pltpu.VMEM((deep, rows, 256), f32),
            pltpu.VMEM(gram_shape, f32),
            pltpu.VMEM((deep, WIDE, 64, 256), bf16),
            pltpu.VMEM((deep, WIDE, 64, 256), bf16),
            pltpu.VMEM((WIDE, deep, 64, 256), bf16),
            pltpu.VMEM((deep, 64, 256), bf16),
            pltpu.VMEM((deep, 64, 256), bf16),
            pltpu.VMEM(send_shape, bf16),
            pltpu.SemaphoreType.DMA((3,)),
            pltpu.SemaphoreType.DMA((3,)),
            pltpu.SemaphoreType.DMA((3, WIDE)),
            pltpu.SemaphoreType.DMA((3, WIDE)),
            pltpu.SemaphoreType.DMA((2, deep)),
            pltpu.SemaphoreType.DMA((2, deep)),
            pltpu.SemaphoreType.DMA((experts,)),
            pltpu.SemaphoreType.DMA((experts,)),
            pltpu.SemaphoreType.DMA,
        ],
        compiler_params=pltpu.CompilerParams(
            collective_id=2, has_side_effects=True, vmem_limit_bytes=40 << 20
        ),
    )(r_part, gram_part.reshape(gram_shape), sketch, coef_t)


def per_device(tokens, cotangent, gate_logit, routes, w_up, w_down, basis, sketch):
    experts = lax.axis_size("expert")
    deep = lax.axis_size("dp") // (WIDE * CORES)
    tok_rows, width_local = tokens.shape
    capacity = min(tok_rows, tok_rows * 4 // experts)
    slot_count = experts * capacity
    gate_first = jax.nn.sigmoid(gate_logit)
    gates = jnp.stack([gate_first, 1.0 - gate_first], axis=1)
    expert_ids = jnp.arange(experts, dtype=jnp.int32)
    chosen = routes[:, :, None] == expert_ids[None, None, :]
    hit_count = jnp.sum(chosen.astype(jnp.int32), axis=1)
    gate_by_expert = jnp.sum(chosen.astype(f32) * gates[:, :, None], axis=1)
    before = jnp.cumsum(hit_count, axis=0) - hit_count
    slot_of = expert_ids[None, :] * capacity + before
    slot_ids = jnp.arange(slot_count, dtype=jnp.int32)
    slot_match = (
        (slot_of[None, :, :] == slot_ids[:, None, None]) & (hit_count[None, :, :] > 0)
    ).astype(f32)
    table = jnp.sum(slot_match, axis=2)
    gate_slot = jnp.sum(slot_match * gate_by_expert[None, :, :], axis=(1, 2))
    table_b = table.astype(bf16)
    both = jnp.concatenate([tokens, cotangent], axis=1)
    picked = jnp.dot(table_b, both, preferred_element_type=f32)
    scale = jnp.where(jnp.arange(2 * width_local)[None, :] < width_local, 1.0, gate_slot[:, None])
    packed = (picked * scale).astype(bf16).reshape(experts, capacity, 2 * width_local)
    arrived = exchange(packed, experts, 0).reshape(slot_count, 2 * width_local).T
    r_part, coef_t, gram_part = gather_compute(
        arrived[:width_local], arrived[width_local:], basis, w_up[0], w_down[0], deep
    )
    hidden_total = w_up.shape[1] * lax.axis_size("dp")
    returned, merged, solved_t = reduce_all(
        r_part, gram_part, sketch[0], coef_t, deep, experts, hidden_total
    )
    token_grad = lax.dot_general(
        table_b,
        returned.reshape(slot_count, 128)[:, :width_local],
        (((0,), (0,)), ((), ())),
        preferred_element_type=f32,
    ).astype(bf16)
    return (token_grad, merged[None], solved_t[None])


def solution(mesh):
    in_specs = (
        P("expert", "dp"),
        P("expert", "dp"),
        P("expert"),
        P("expert", None),
        P("expert", "dp", None),
        P("expert", "dp", None),
        P("dp", None),
        P("expert", None, None),
    )
    out_specs = (P("expert", "dp"), P("expert", None, None), P("expert", "dp", None))
    return jax.shard_map(
        per_device, mesh=mesh, in_specs=in_specs, out_specs=out_specs, check_vma=False
    )
```

```python
import functools

import jax
import jax.numpy as jnp
from jax import lax
from jax.experimental import pallas as pl
from jax.experimental.pallas import tpu as pltpu
from jax.sharding import PartitionSpec as P

decay_rate = 0.9
damping = 1.0
highest = lax.Precision.HIGHEST
MESH = pl.DeviceIdType.MESH
CORES = 2
WIDE = 4
bf16 = jnp.bfloat16
f32 = jnp.float32
VMEM = pl.BlockSpec(memory_space=pltpu.VMEM)
HBM = pl.BlockSpec(memory_space=pltpu.HBM)


def greet(axis, peers):
    barrier = pltpu.get_barrier_semaphore()
    for peer in peers:
        pl.semaphore_signal(barrier, inc=1, device_id={axis: peer}, device_id_type=MESH)
    pl.semaphore_wait(barrier, len(peers))


def remote(src, dst, send, recv, axis, peer):
    copy = pltpu.make_async_remote_copy(
        src_ref=src,
        dst_ref=dst,
        send_sem=send,
        recv_sem=recv,
        device_id={axis: peer},
        device_id_type=MESH,
    )
    copy.start()
    return copy


def exchange_kernel(n, src, dst, send, recv, own):
    me = lax.axis_index("expert")
    peers = [lax.rem(me + k, n) for k in range(1, n)]
    greet("expert", peers)
    copies = [
        remote(src.at[peer], dst.at[me], send.at[k], recv.at[k], "expert", peer)
        for k, peer in enumerate(peers)
    ]
    mine = pltpu.make_async_copy(src.at[me], dst.at[me], own)
    mine.start()
    for copy in copies:
        copy.wait()
    mine.wait()


def exchange(value, n, number):
    return pl.pallas_call(
        functools.partial(exchange_kernel, n),
        out_shape=jax.ShapeDtypeStruct(value.shape, value.dtype),
        in_specs=[VMEM],
        out_specs=VMEM,
        scratch_shapes=[
            pltpu.SemaphoreType.DMA((n,)),
            pltpu.SemaphoreType.DMA((n,)),
            pltpu.SemaphoreType.DMA,
        ],
        compiler_params=pltpu.CompilerParams(
            collective_id=number, has_side_effects=True, vmem_limit_bytes=4 << 20
        ),
    )(value)


def place(deep):
    me = lax.axis_index("dp")
    core = lax.rem(me, CORES)
    chip = me // CORES
    return chip // WIDE, lax.rem(chip, WIDE), core


def index_of(z, x, core):
    return (z * WIDE + x) * CORES + core


def gather_kernel(
    deep, x_in, dy_in, basis_in, up_hbm, down_hbm, r_out, c_out, gram_out,
    xs, dys, bases, up, down, hid, back, proj, sent, got, ring_send, ring_recv, share_send, share_recv,
    early_send, early_recv,
):
    z, x, core = place(deep)
    other = 1 - core
    partner = index_of(z, x, other)
    sizes = {"z": deep, "x": WIDE}
    spot = {"z": z, "x": x}

    def near(axis, step):
        at = lax.rem(spot[axis] + step + sizes[axis], sizes[axis])
        return index_of(at, x, core) if axis == "z" else index_of(z, at, core)

    fetch_up = pltpu.make_async_copy(up_hbm, up, got.at[0])
    fetch_down = pltpu.make_async_copy(down_hbm, down, got.at[1])
    fetch_up.start()
    fetch_down.start()
    greet("dp", [near("z", 1), near("z", -1), near("x", 1), near("x", -1), partner])

    full = [xs, dys, bases]
    starts = [x_in, dy_in, basis_in]
    orders = [("z", "x"), ("x", "z"), ("z", "x")]
    own = []
    for t in range(3):
        copy = pltpu.make_async_copy(starts[t], full[t].at[z, x, core], sent.at[t])
        copy.start()
        own.append(copy)
    sends = []
    flows = []

    def block(t, axis, at, half=None):
        rows = slice(None) if half is None else pl.ds(half * 32, 32)
        return full[t].at[at, x, core, rows] if axis == "z" else full[t].at[z, at, core, rows]

    def slab(t, axis, at, half=None):
        if axis == "x":
            part = slice(None) if half is None else pl.ds(half * (deep // 2), deep // 2)
            return full[t].at[part, at, core]
        part = slice(None) if half is None else pl.ds(half * (WIDE // 2), WIDE // 2)
        return full[t].at[at, part, core]

    def ring_step(t, phase, axis, step, view):
        last = sizes[axis] // 2
        copies = []
        for way, sign in enumerate((1, -1)):
            at = lax.rem(spot[axis] - sign * (step - 1) + sizes[axis], sizes[axis])
            piece = view(t, axis, at, way if step == last else None)
            source = piece
            if phase == 0 and step == 1:
                source = starts[t] if step != last else starts[t].at[pl.ds(way * 32, 32)]
            copies.append(
                remote(
                    source, piece, ring_send.at[t, phase, way, step - 1],
                    ring_recv.at[t, phase, way, step - 1], "dp", near(axis, sign),
                )
            )
        sends.extend(copies)
        return copies

    shares = []

    def share(t, axis, at):
        piece = slab(t, axis, at)
        number = 0
        for old in shares:
            number += old[0] == t
        copy = remote(
            piece, piece, share_send.at[t, number], share_recv.at[t, number], "dp", partner
        )
        shares.append((t, copy))

    def stages(t):
        first, second = orders[t]
        n = sizes[second]
        count = sizes[first]
        early = []

        def pass_on(at, source=None):
            piece = block(t, first, at)
            number = len(early) // 2
            for way, sign in enumerate((1, -1)):
                early.append(
                    remote(
                        piece if source is None else source, piece,
                        early_send.at[t, way, number], early_recv.at[t, way, number],
                        "dp", near(second, sign),
                    )
                )

        for step in range(1, count // 2 + 1):
            copies = ring_step(t, 0, first, step, block)
            if step == 1 and n > 2:
                pass_on(spot[first], starts[t])
            yield
            for copy in copies:
                copy.wait_recv()
            if n > 2:
                pass_on(lax.rem(spot[first] - step + count, count))
                if step < count // 2:
                    pass_on(lax.rem(spot[first] + step, count))
        own[t].wait()
        at = spot[second]
        sends.extend(early)
        copies = early if n > 2 else ring_step(t, 1, second, 1, slab)
        share(t, second, at)
        yield
        for step in range(1, n // 2):
            for copy in copies:
                copy.wait_recv()
            copies = ring_step(t, 1, second, step + 1, slab)
            share(t, second, lax.rem(at - step + n, n))
            share(t, second, lax.rem(at + step, n))
            yield
        for copy in copies:
            copy.wait_recv()
        share(t, second, lax.rem(at + n // 2, n))

    flows = [stages(t) for t in range(3)]
    while flows:
        for flow in list(flows):
            if next(flow, flow) is flow:
                flows.remove(flow)
    fetch_up.wait()
    fetch_down.wait()
    for copy in sends:
        copy.wait_send()
    for _, copy in shares:
        copy.wait()

    chunk = WIDE * CORES * 64
    hid[...] = jnp.zeros_like(hid)
    back[...] = jnp.zeros_like(back)
    proj[...] = jnp.zeros_like(proj)
    turned = (((0,), (0,)), ((), ()))

    def forward(at, carry):
        columns = pl.ds(pl.multiple_of(at * chunk, chunk), chunk)
        x_part = xs[at].reshape(chunk, 256)
        dy_part = dys[at].reshape(chunk, 256)
        basis_part = bases[at].reshape(chunk, 256)
        hid[...] += jnp.dot(up[:, columns], x_part, preferred_element_type=f32)
        back[...] += jnp.dot(down[:, columns], dy_part, preferred_element_type=f32)
        proj[...] += lax.dot_general(x_part, basis_part, turned, preferred_element_type=f32)
        return carry

    lax.fori_loop(0, deep, forward, 0)
    hidden = hid[...]
    sigma = jax.nn.sigmoid(hidden)
    grad = (back[...] * sigma * (1.0 + hidden * (1.0 - sigma))).astype(bf16)
    coef = jnp.dot(grad, proj[...].astype(bf16), preferred_element_type=f32)
    c_out[...] = coef
    gram_out[...] = lax.dot_general(
        coef, coef, turned, precision=highest, preferred_element_type=f32
    )

    def rows(at, carry):
        columns = pl.ds(pl.multiple_of(at * chunk, chunk), chunk)
        part = lax.dot_general(up[:, columns], grad, turned, preferred_element_type=f32)
        r_out[at] = part.astype(bf16).reshape(WIDE, CORES, 64, 256)
        return carry

    lax.fori_loop(0, deep, rows, 0)


def gather_compute(x_t, dy_t, basis, up, down, deep):
    units, width = up.shape
    blocks = (deep, WIDE, CORES, 64, 256)
    steps = max(deep, WIDE)
    return pl.pallas_call(
        functools.partial(gather_kernel, deep),
        out_shape=(
            jax.ShapeDtypeStruct(blocks, bf16),
            jax.ShapeDtypeStruct((units, 256), f32),
            jax.ShapeDtypeStruct((256, 256), f32),
        ),
        in_specs=[VMEM, VMEM, VMEM, HBM, HBM],
        out_specs=(VMEM, VMEM, VMEM),
        scratch_shapes=[
            pltpu.VMEM(blocks, bf16),
            pltpu.VMEM(blocks, bf16),
            pltpu.VMEM(blocks, bf16),
            pltpu.VMEM((units, width), bf16),
            pltpu.VMEM((units, width), bf16),
            pltpu.VMEM((units, 256), f32),
            pltpu.VMEM((units, 256), f32),
            pltpu.VMEM((256, 256), f32),
            pltpu.SemaphoreType.DMA((3,)),
            pltpu.SemaphoreType.DMA((2,)),
            pltpu.SemaphoreType.DMA((3, 2, 2, steps // 2)),
            pltpu.SemaphoreType.DMA((3, 2, 2, steps // 2)),
            pltpu.SemaphoreType.DMA((3, steps)),
            pltpu.SemaphoreType.DMA((3, steps)),
            pltpu.SemaphoreType.DMA((3, 2, steps)),
            pltpu.SemaphoreType.DMA((3, 2, steps)),
        ],
        compiler_params=pltpu.CompilerParams(
            collective_id=1, has_side_effects=True, vmem_limit_bytes=52 << 20
        ),
    )(x_t, dy_t, basis, up, down)


def eliminate(matrix, rounds):
    n, group = 128, 16
    lane = lax.broadcasted_iota(jnp.int32, (1, n), 1)
    row = lax.broadcasted_iota(jnp.int32, (group, n), 0)

    def pivots(_, parts):
        top, rest = parts
        for k in range(0, group, 2):
            first = jnp.broadcast_to(top[:, k : k + 1], (group, n))
            second = jnp.broadcast_to(top[:, k + 1 : k + 2], (group, n))
            first_rest = jnp.broadcast_to(rest[:, k : k + 1], (n - group, n))
            second_rest = jnp.broadcast_to(rest[:, k + 1 : k + 2], (n - group, n))
            a, b, d = first[k : k + 1], first[k + 1 : k + 2], second[k + 1 : k + 2]
            a_inv = 1.0 / a
            slope = b * a_inv
            d_inv = 1.0 / (d - b * slope)
            p12 = -slope * d_inv
            p11 = a_inv - slope * p12
            at_first, at_second = lane == k, lane == k + 1
            row_a, row_b = top[k : k + 1], top[k + 1 : k + 2]
            u_a = p11 * row_a + p12 * row_b
            u_b = p12 * row_a + d_inv * row_b
            u_a = jnp.where(at_first, p11, jnp.where(at_second, p12, u_a))
            u_b = jnp.where(at_first, p12, jnp.where(at_second, d_inv, u_b))
            inside = at_first | at_second
            rest = jnp.where(inside, 0.0, rest) - first_rest * u_a - second_rest * u_b
            top = jnp.where(inside, 0.0, top) - first * u_a - second * u_b
            top = jnp.where(row == k, u_a, jnp.where(row == k + 1, u_b, top))
        turned = pltpu.roll(jnp.concatenate([rest, top], axis=0), n - group, 1)
        return turned[:group], turned[group:]

    top, rest = lax.fori_loop(0, rounds, pivots, (matrix[:group], matrix[group:]))
    return jnp.concatenate([top, rest], axis=0)


def exact(left, right, dims=(((1,), (0,)), ((), ()))):
    return lax.dot_general(left, right, dims, precision=highest, preferred_element_type=f32)


def reduce_kernel(
    deep, experts, hidden_total, r_in, gram_in, sketch_in, coef_in, back_out, merged_out, solved_out,
    g0, gsum, gx, gz, gram_out, r0, rsum, rx, r1, rz, ready,
    core_send, core_recv, x_send, x_recv, z_send, z_recv, y_send, y_recv, y_own,
):
    z, x, core = place(deep)
    me_y = lax.axis_index("expert")
    other = 1 - core
    partner = index_of(z, x, other)
    x_at = [lax.rem(x + k, WIDE) for k in range(1, WIDE)]
    z_at = [lax.rem(z + k, deep) for k in range(1, deep)]
    y_at = [lax.rem(me_y + k, experts) for k in range(1, experts)]
    x_peers = [index_of(z, at, core) for at in x_at]
    z_peers = [index_of(at, x, core) for at in z_at]
    barrier = pltpu.get_barrier_semaphore()
    for peer in y_at:
        pl.semaphore_signal(barrier, inc=1, device_id={"expert": peer}, device_id_type=MESH)
    for peer in [partner] + x_peers + z_peers:
        pl.semaphore_signal(barrier, inc=1, device_id={"dp": peer}, device_id_type=MESH)
    pl.semaphore_wait(barrier, 1 + len(x_peers) + len(z_peers) + len(y_at))

    def to_core(number, src, dst):
        return remote(src, dst, core_send.at[number], core_recv.at[number], "dp", partner)

    def along_x(number, pairs):
        return [
            remote(src, dst, x_send.at[number, k], x_recv.at[number, k], "dp", x_peers[k])
            for k, (src, dst) in enumerate(pairs)
        ]

    def along_z(number, pairs):
        return [
            remote(src, dst, z_send.at[number, k], z_recv.at[number, k], "dp", z_peers[k])
            for k, (src, dst) in enumerate(pairs)
        ]

    gram_core = to_core(0, gram_in.at[other], g0)
    r_core = to_core(1, r_in.at[:, :, other], r0)

    gram_core.wait_recv()
    gsum[...] = gram_in[core] + g0[...]
    gram_x = along_x(0, [(gsum.at[at], gx.at[x]) for at in x_at])

    r_core.wait_recv()

    def add_core(at, carry):
        rsum[at] = (r_in[at, :, core].astype(f32) + r0[at].astype(f32)).astype(bf16)
        return carry

    lax.fori_loop(0, deep, add_core, 0)

    for copy in gram_x:
        copy.wait_recv()
    total = gsum[x]
    for at in x_at:
        total = total + gx[at]
    gz[z] = total
    gram_z = along_z(0, [(gz.at[z], gz.at[z]) for _ in z_at])
    r_x = along_x(1, [(rsum.at[:, at], rx.at[x]) for at in x_at])

    for copy in gram_z:
        copy.wait_recv()
    total = gz[0]
    for at in range(1, deep):
        total = total + gz[at]
    gram_out[core, x] = total
    gram_back = along_x(2, [(gram_out.at[core, x], gram_out.at[core, x]) for _ in x_at])
    for copy in gram_back:
        copy.wait_recv()
    gram_last = to_core(2, gram_out.at[core], gram_out.at[core])
    gram_last.wait_recv()

    merged = decay_rate * sketch_in[...] + gram_out[...].reshape(256, 256) / hidden_total
    merged_out[...] = merged
    half = 128
    eye = (
        lax.broadcasted_iota(jnp.int32, (half, half), 0)
        == lax.broadcasted_iota(jnp.int32, (half, half), 1)
    ).astype(f32) * damping
    corner = merged[:half, half:]
    upper = eliminate(merged[:half, :half] + eye, 8)
    ratio = exact(upper, corner)
    lower = merged[half:, half:] + eye - exact(merged[half:, :half], ratio)

    for copy in r_x:
        copy.wait_recv()

    def add_x(at, carry):
        part = rsum[at, x].astype(f32)
        for peer in x_at:
            part = part + rx[peer, at].astype(f32)
        r1[at] = part.astype(bf16)
        return carry

    lax.fori_loop(0, deep, add_x, 0)
    r_z = along_z(1, [(r1.at[at], rz.at[z]) for at in z_at])

    left, right = coef_in[:, :half], coef_in[:, half:]
    right = right - exact(left, ratio)
    left = exact(left, upper)
    lower = eliminate(lower, 4)
    for copy in r_z:
        copy.wait_recv()
    part = r1[z].astype(f32)
    for at in z_at:
        part = part + rz[at].astype(f32)
    part = jnp.concatenate([part, jnp.zeros_like(part)], axis=0)
    ready[...] = part.T.astype(bf16).reshape(ready.shape)
    r_y = [
        remote(ready.at[at], back_out.at[me_y], y_send.at[k], y_recv.at[k], "expert", at)
        for k, at in enumerate(y_at)
    ]
    mine = pltpu.make_async_copy(ready.at[me_y], back_out.at[me_y], y_own)
    mine.start()

    right = exact(right, eliminate(lower, 4))
    solved_out[:, half:] = right * damping
    left = left - exact(right, ratio, (((1,), (1,)), ((), ())))
    solved_out[:, :half] = left * damping

    for copy in r_y:
        copy.wait_recv()
    mine.wait()
    for copy in [gram_core, r_core, gram_last] + gram_x + r_x + gram_back + gram_z + r_z + r_y:
        copy.wait_send()


def reduce_all(r_part, gram_part, sketch, coef_t, deep, experts, hidden_total):
    rows = 256 // (CORES * WIDE)
    gram_shape = (CORES, WIDE, rows, 256)
    send_shape = (experts, 256 // experts, 128)
    return pl.pallas_call(
        functools.partial(reduce_kernel, deep, experts, hidden_total),
        out_shape=(
            jax.ShapeDtypeStruct(send_shape, bf16),
            jax.ShapeDtypeStruct((256, 256), f32),
            jax.ShapeDtypeStruct(coef_t.shape, f32),
        ),
        in_specs=[VMEM] * 4,
        out_specs=(VMEM,) * 3,
        scratch_shapes=[
            pltpu.VMEM((WIDE, rows, 256), f32),
            pltpu.VMEM((WIDE, rows, 256), f32),
            pltpu.VMEM((WIDE, rows, 256), f32),
            pltpu.VMEM((deep, rows, 256), f32),
            pltpu.VMEM(gram_shape, f32),
            pltpu.VMEM((deep, WIDE, 64, 256), bf16),
            pltpu.VMEM((deep, WIDE, 64, 256), bf16),
            pltpu.VMEM((WIDE, deep, 64, 256), bf16),
            pltpu.VMEM((deep, 64, 256), bf16),
            pltpu.VMEM((deep, 64, 256), bf16),
            pltpu.VMEM(send_shape, bf16),
            pltpu.SemaphoreType.DMA((3,)),
            pltpu.SemaphoreType.DMA((3,)),
            pltpu.SemaphoreType.DMA((3, WIDE)),
            pltpu.SemaphoreType.DMA((3, WIDE)),
            pltpu.SemaphoreType.DMA((2, deep)),
            pltpu.SemaphoreType.DMA((2, deep)),
            pltpu.SemaphoreType.DMA((experts,)),
            pltpu.SemaphoreType.DMA((experts,)),
            pltpu.SemaphoreType.DMA,
        ],
        compiler_params=pltpu.CompilerParams(
            collective_id=2, has_side_effects=True, vmem_limit_bytes=40 << 20
        ),
    )(r_part, gram_part.reshape(gram_shape), sketch, coef_t)


def per_device(tokens, cotangent, gate_logit, routes, w_up, w_down, basis, sketch):
    experts = lax.axis_size("expert")
    deep = lax.axis_size("dp") // (WIDE * CORES)
    tok_rows, width_local = tokens.shape
    capacity = min(tok_rows, tok_rows * 4 // experts)
    slot_count = experts * capacity
    gate_first = jax.nn.sigmoid(gate_logit)
    gates = jnp.stack([gate_first, 1.0 - gate_first], axis=1)
    expert_ids = jnp.arange(experts, dtype=jnp.int32)
    chosen = routes[:, :, None] == expert_ids[None, None, :]
    hit_count = jnp.sum(chosen.astype(jnp.int32), axis=1)
    gate_by_expert = jnp.sum(chosen.astype(f32) * gates[:, :, None], axis=1)
    before = jnp.cumsum(hit_count, axis=0) - hit_count
    slot_of = expert_ids[None, :] * capacity + before
    slot_ids = jnp.arange(slot_count, dtype=jnp.int32)
    slot_match = (
        (slot_of[None, :, :] == slot_ids[:, None, None]) & (hit_count[None, :, :] > 0)
    ).astype(f32)
    table = jnp.sum(slot_match, axis=2)
    gate_slot = jnp.sum(slot_match * gate_by_expert[None, :, :], axis=(1, 2))
    table_b = table.astype(bf16)
    both = jnp.concatenate([tokens, cotangent], axis=1)
    picked = jnp.dot(table_b, both, preferred_element_type=f32)
    scale = jnp.where(jnp.arange(2 * width_local)[None, :] < width_local, 1.0, gate_slot[:, None])
    packed = (picked * scale).astype(bf16).reshape(experts, capacity, 2 * width_local)
    arrived = exchange(packed, experts, 0).reshape(slot_count, 2 * width_local).T
    r_part, coef_t, gram_part = gather_compute(
        arrived[:width_local], arrived[width_local:], basis, w_up[0], w_down[0], deep
    )
    hidden_total = w_up.shape[1] * lax.axis_size("dp")
    returned, merged, solved_t = reduce_all(
        r_part, gram_part, sketch[0], coef_t, deep, experts, hidden_total
    )
    token_grad = lax.dot_general(
        table_b,
        returned.reshape(slot_count, 128)[:, :width_local],
        (((0,), (0,)), ((), ())),
        preferred_element_type=f32,
    ).astype(bf16)
    return (token_grad, merged[None], solved_t[None])


def solution(mesh):
    in_specs = (
        P("expert", "dp"),
        P("expert", "dp"),
        P("expert"),
        P("expert", None),
        P("expert", "dp", None),
        P("expert", "dp", None),
        P("dp", None),
        P("expert", None, None),
    )
    out_specs = (P("expert", "dp"), P("expert", None, None), P("expert", "dp", None))
    return jax.shard_map(
        per_device, mesh=mesh, in_specs=in_specs, out_specs=out_specs, check_vma=False
    )
```

```python
import functools

import jax
import jax.numpy as jnp
from jax import lax
from jax.experimental import pallas as pl
from jax.experimental.pallas import tpu as pltpu
from jax.sharding import PartitionSpec as P

decay_rate = 0.9
damping = 1.0
highest = lax.Precision.HIGHEST
MESH = pl.DeviceIdType.MESH
CORES = 2
WIDE = 4
bf16 = jnp.bfloat16
f32 = jnp.float32
VMEM = pl.BlockSpec(memory_space=pltpu.VMEM)
HBM = pl.BlockSpec(memory_space=pltpu.HBM)


def greet(axis, peers):
    barrier = pltpu.get_barrier_semaphore()
    for peer in peers:
        pl.semaphore_signal(barrier, inc=1, device_id={axis: peer}, device_id_type=MESH)
    pl.semaphore_wait(barrier, len(peers))


def remote(src, dst, send, recv, axis, peer):
    copy = pltpu.make_async_remote_copy(
        src_ref=src,
        dst_ref=dst,
        send_sem=send,
        recv_sem=recv,
        device_id={axis: peer},
        device_id_type=MESH,
    )
    copy.start()
    return copy


def exchange_kernel(n, src, dst, send, recv, own):
    me = lax.axis_index("expert")
    peers = [lax.rem(me + k, n) for k in range(1, n)]
    greet("expert", peers)
    copies = [
        remote(src.at[peer], dst.at[me], send.at[k], recv.at[k], "expert", peer)
        for k, peer in enumerate(peers)
    ]
    mine = pltpu.make_async_copy(src.at[me], dst.at[me], own)
    mine.start()
    for copy in copies:
        copy.wait()
    mine.wait()


def exchange(value, n, number):
    return pl.pallas_call(
        functools.partial(exchange_kernel, n),
        out_shape=jax.ShapeDtypeStruct(value.shape, value.dtype),
        in_specs=[VMEM],
        out_specs=VMEM,
        scratch_shapes=[
            pltpu.SemaphoreType.DMA((n,)),
            pltpu.SemaphoreType.DMA((n,)),
            pltpu.SemaphoreType.DMA,
        ],
        compiler_params=pltpu.CompilerParams(
            collective_id=number, has_side_effects=True, vmem_limit_bytes=4 << 20
        ),
    )(value)


def place(deep):
    me = lax.axis_index("dp")
    core = lax.rem(me, CORES)
    chip = me // CORES
    return chip // WIDE, lax.rem(chip, WIDE), core


def index_of(z, x, core):
    return (z * WIDE + x) * CORES + core


def gather_kernel(
    deep, x_in, dy_in, basis_in, up_hbm, down_hbm, r_out, c_out, gram_out,
    xs, dys, bases, up, down, hid, back, proj, sent, got, ring_send, ring_recv, share_send, share_recv,
    early_send, early_recv,
):
    z, x, core = place(deep)
    other = 1 - core
    partner = index_of(z, x, other)
    sizes = {"z": deep, "x": WIDE}
    spot = {"z": z, "x": x}

    def near(axis, step):
        at = lax.rem(spot[axis] + step + sizes[axis], sizes[axis])
        return index_of(at, x, core) if axis == "z" else index_of(z, at, core)

    fetch_up = pltpu.make_async_copy(up_hbm, up, got.at[0])
    fetch_down = pltpu.make_async_copy(down_hbm, down, got.at[1])
    fetch_up.start()
    fetch_down.start()
    greet("dp", [near("z", 1), near("z", -1), near("x", 1), near("x", -1), partner])

    full = [xs, dys, bases]
    starts = [x_in, dy_in, basis_in]
    orders = [("z", "x"), ("x", "z"), ("z", "x")]
    own = []
    for t in range(3):
        copy = pltpu.make_async_copy(starts[t], full[t].at[z, x, core], sent.at[t])
        copy.start()
        own.append(copy)
    sends = []
    flows = []

    def block(t, axis, at, half=None):
        rows = slice(None) if half is None else pl.ds(half * 32, 32)
        return full[t].at[at, x, core, rows] if axis == "z" else full[t].at[z, at, core, rows]

    def slab(t, axis, at, half=None):
        if axis == "x":
            part = slice(None) if half is None else pl.ds(half * (deep // 2), deep // 2)
            return full[t].at[part, at, core]
        part = slice(None) if half is None else pl.ds(half * (WIDE // 2), WIDE // 2)
        return full[t].at[at, part, core]

    def ring_step(t, phase, axis, step, view):
        last = sizes[axis] // 2
        copies = []
        for way, sign in enumerate((1, -1)):
            at = lax.rem(spot[axis] - sign * (step - 1) + sizes[axis], sizes[axis])
            piece = view(t, axis, at, way if step == last else None)
            source = piece
            if phase == 0 and step == 1:
                source = starts[t] if step != last else starts[t].at[pl.ds(way * 32, 32)]
            copies.append(
                remote(
                    source, piece, ring_send.at[t, phase, way, step - 1],
                    ring_recv.at[t, phase, way, step - 1], "dp", near(axis, sign),
                )
            )
        sends.extend(copies)
        return copies

    shares = []

    def share(t, axis, at):
        piece = slab(t, axis, at)
        number = 0
        for old in shares:
            number += old[0] == t
        copy = remote(
            piece, piece, share_send.at[t, number], share_recv.at[t, number], "dp", partner
        )
        shares.append((t, copy))

    def stages(t):
        first, second = orders[t]
        n = sizes[second]
        count = sizes[first]
        early = []

        def pass_on(at, source=None):
            piece = block(t, first, at)
            number = len(early) // 2
            for way, sign in enumerate((1, -1)):
                early.append(
                    remote(
                        piece if source is None else source, piece,
                        early_send.at[t, way, number], early_recv.at[t, way, number],
                        "dp", near(second, sign),
                    )
                )

        for step in range(1, count // 2 + 1):
            copies = ring_step(t, 0, first, step, block)
            if step == 1 and n > 2:
                pass_on(spot[first], starts[t])
            yield
            for copy in copies:
                copy.wait_recv()
            if n > 2:
                pass_on(lax.rem(spot[first] - step + count, count))
                if step < count // 2:
                    pass_on(lax.rem(spot[first] + step, count))
        own[t].wait()
        at = spot[second]
        sends.extend(early)
        copies = early if n > 2 else ring_step(t, 1, second, 1, slab)
        share(t, second, at)
        yield
        for step in range(1, n // 2):
            for copy in copies:
                copy.wait_recv()
            copies = ring_step(t, 1, second, step + 1, slab)
            share(t, second, lax.rem(at - step + n, n))
            share(t, second, lax.rem(at + step, n))
            yield
        for copy in copies:
            copy.wait_recv()
        share(t, second, lax.rem(at + n // 2, n))

    flows = [stages(t) for t in range(3)]
    while flows:
        for flow in list(flows):
            if next(flow, flow) is flow:
                flows.remove(flow)
    fetch_up.wait()
    fetch_down.wait()
    for copy in sends:
        copy.wait_send()
    for _, copy in shares:
        copy.wait()

    chunk = WIDE * CORES * 64
    hid[...] = jnp.zeros_like(hid)
    back[...] = jnp.zeros_like(back)
    proj[...] = jnp.zeros_like(proj)
    turned = (((0,), (0,)), ((), ()))

    def forward(at, carry):
        columns = pl.ds(pl.multiple_of(at * chunk, chunk), chunk)
        x_part = xs[at].reshape(chunk, 256)
        dy_part = dys[at].reshape(chunk, 256)
        basis_part = bases[at].reshape(chunk, 256)
        hid[...] += jnp.dot(up[:, columns], x_part, preferred_element_type=f32)
        back[...] += jnp.dot(down[:, columns], dy_part, preferred_element_type=f32)
        proj[...] += lax.dot_general(x_part, basis_part, turned, preferred_element_type=f32)
        return carry

    lax.fori_loop(0, deep, forward, 0)
    hidden = hid[...]
    sigma = jax.nn.sigmoid(hidden)
    grad = (back[...] * sigma * (1.0 + hidden * (1.0 - sigma))).astype(bf16)
    coef = jnp.dot(grad, proj[...].astype(bf16), preferred_element_type=f32)
    c_out[...] = coef
    gram_out[...] = lax.dot_general(
        coef, coef, turned, precision=highest, preferred_element_type=f32
    )

    def rows(at, carry):
        columns = pl.ds(pl.multiple_of(at * chunk, chunk), chunk)
        part = lax.dot_general(up[:, columns], grad, turned, preferred_element_type=f32)
        r_out[at] = part.astype(bf16).reshape(WIDE, CORES, 64, 256)
        return carry

    lax.fori_loop(0, deep, rows, 0)


def gather_compute(x_t, dy_t, basis, up, down, deep):
    units, width = up.shape
    blocks = (deep, WIDE, CORES, 64, 256)
    steps = max(deep, WIDE)
    return pl.pallas_call(
        functools.partial(gather_kernel, deep),
        out_shape=(
            jax.ShapeDtypeStruct(blocks, bf16),
            jax.ShapeDtypeStruct((units, 256), f32),
            jax.ShapeDtypeStruct((256, 256), f32),
        ),
        in_specs=[VMEM, VMEM, VMEM, HBM, HBM],
        out_specs=(VMEM, VMEM, VMEM),
        scratch_shapes=[
            pltpu.VMEM(blocks, bf16),
            pltpu.VMEM(blocks, bf16),
            pltpu.VMEM(blocks, bf16),
            pltpu.VMEM((units, width), bf16),
            pltpu.VMEM((units, width), bf16),
            pltpu.VMEM((units, 256), f32),
            pltpu.VMEM((units, 256), f32),
            pltpu.VMEM((256, 256), f32),
            pltpu.SemaphoreType.DMA((3,)),
            pltpu.SemaphoreType.DMA((2,)),
            pltpu.SemaphoreType.DMA((3, 2, 2, steps // 2)),
            pltpu.SemaphoreType.DMA((3, 2, 2, steps // 2)),
            pltpu.SemaphoreType.DMA((3, steps)),
            pltpu.SemaphoreType.DMA((3, steps)),
            pltpu.SemaphoreType.DMA((3, 2, steps)),
            pltpu.SemaphoreType.DMA((3, 2, steps)),
        ],
        compiler_params=pltpu.CompilerParams(
            collective_id=1, has_side_effects=True, vmem_limit_bytes=52 << 20
        ),
    )(x_t, dy_t, basis, up, down)


def eliminate(matrix, rounds):
    n, group = 128, 16
    lane = lax.broadcasted_iota(jnp.int32, (1, n), 1)
    row = lax.broadcasted_iota(jnp.int32, (group, n), 0)

    def pivots(_, parts):
        top, rest = parts
        for k in range(0, group, 2):
            first = jnp.broadcast_to(top[:, k : k + 1], (group, n))
            second = jnp.broadcast_to(top[:, k + 1 : k + 2], (group, n))
            first_rest = jnp.broadcast_to(rest[:, k : k + 1], (n - group, n))
            second_rest = jnp.broadcast_to(rest[:, k + 1 : k + 2], (n - group, n))
            a, b, d = first[k : k + 1], first[k + 1 : k + 2], second[k + 1 : k + 2]
            a_inv = 1.0 / a
            slope = b * a_inv
            d_inv = 1.0 / (d - b * slope)
            p12 = -slope * d_inv
            p11 = a_inv - slope * p12
            at_first, at_second = lane == k, lane == k + 1
            row_a, row_b = top[k : k + 1], top[k + 1 : k + 2]
            u_a = p11 * row_a + p12 * row_b
            u_b = p12 * row_a + d_inv * row_b
            u_a = jnp.where(at_first, p11, jnp.where(at_second, p12, u_a))
            u_b = jnp.where(at_first, p12, jnp.where(at_second, d_inv, u_b))
            inside = at_first | at_second
            rest = jnp.where(inside, 0.0, rest) - first_rest * u_a - second_rest * u_b
            top = jnp.where(inside, 0.0, top) - first * u_a - second * u_b
            top = jnp.where(row == k, u_a, jnp.where(row == k + 1, u_b, top))
        turned = pltpu.roll(jnp.concatenate([rest, top], axis=0), n - group, 1)
        return turned[:group], turned[group:]

    top, rest = lax.fori_loop(0, rounds, pivots, (matrix[:group], matrix[group:]))
    return jnp.concatenate([top, rest], axis=0)


def exact(left, right, dims=(((1,), (0,)), ((), ()))):
    return lax.dot_general(left, right, dims, precision=highest, preferred_element_type=f32)


def reduce_kernel(
    deep, experts, hidden_total, r_in, gram_in, sketch_in, coef_in, back_out, merged_out, solved_out,
    g0, gsum, gx, gz, gram_out, r0, rsum, rx, r1, rz, ready,
    core_send, core_recv, x_send, x_recv, z_send, z_recv, y_send, y_recv, y_own,
):
    z, x, core = place(deep)
    me_y = lax.axis_index("expert")
    other = 1 - core
    partner = index_of(z, x, other)
    x_at = [lax.rem(x + k, WIDE) for k in range(1, WIDE)]
    z_at = [lax.rem(z + k, deep) for k in range(1, deep)]
    y_at = [lax.rem(me_y + k, experts) for k in range(1, experts)]
    x_peers = [index_of(z, at, core) for at in x_at]
    z_peers = [index_of(at, x, core) for at in z_at]
    barrier = pltpu.get_barrier_semaphore()
    for peer in y_at:
        pl.semaphore_signal(barrier, inc=1, device_id={"expert": peer}, device_id_type=MESH)
    cross_peers = [index_of(z, at, other) for at in x_at]
    for peer in [partner] + x_peers + cross_peers + z_peers:
        pl.semaphore_signal(barrier, inc=1, device_id={"dp": peer}, device_id_type=MESH)
    pl.semaphore_wait(barrier, 1 + 2 * len(x_peers) + len(z_peers) + len(y_at))

    def to_core(number, src, dst):
        return remote(src, dst, core_send.at[number], core_recv.at[number], "dp", partner)

    def along_x(number, pairs):
        return [
            remote(src, dst, x_send.at[number, k], x_recv.at[number, k], "dp", x_peers[k])
            for k, (src, dst) in enumerate(pairs)
        ]

    def along_z(number, pairs):
        return [
            remote(src, dst, z_send.at[number, k], z_recv.at[number, k], "dp", z_peers[k])
            for k, (src, dst) in enumerate(pairs)
        ]

    gram_core = to_core(0, gram_in.at[other], g0)
    r_core = to_core(1, r_in.at[:, :, other], r0)

    gram_core.wait_recv()
    gsum[...] = gram_in[core] + g0[...]
    gram_x = along_x(0, [(gsum.at[at], gx.at[x]) for at in x_at])

    for copy in gram_x:
        copy.wait_recv()
    total = gsum[x]
    for at in x_at:
        total = total + gx[at]
    gz[z] = total
    gram_z = along_z(0, [(gz.at[z], gz.at[z]) for _ in z_at])

    r_core.wait_recv()

    def add_core(at, carry):
        rsum[at] = (r_in[at, :, core].astype(f32) + r0[at].astype(f32)).astype(bf16)
        return carry

    lax.fori_loop(0, deep, add_core, 0)


    for copy in gram_z:
        copy.wait_recv()
    total = gz[0]
    for at in range(1, deep):
        total = total + gz[at]
    gram_out[core, x] = total
    gram_back = along_x(2, [(gram_out.at[core, x], gram_out.at[core, x]) for _ in x_at])
    piece = gram_out.at[core, x]
    gram_back += [
        remote(piece, piece, x_send.at[3, k], x_recv.at[3, k], "dp", peer)
        for k, peer in enumerate(cross_peers)
    ]
    gram_last = to_core(2, piece, piece)
    r_x = along_x(1, [(rsum.at[:, at], rx.at[x]) for at in x_at])
    gram_last.wait_recv()
    for copy in gram_back:
        copy.wait_recv()

    merged = decay_rate * sketch_in[...] + gram_out[...].reshape(256, 256) / hidden_total
    merged_out[...] = merged
    half = 128
    eye = (
        lax.broadcasted_iota(jnp.int32, (half, half), 0)
        == lax.broadcasted_iota(jnp.int32, (half, half), 1)
    ).astype(f32) * damping
    corner = merged[:half, half:]
    upper = eliminate(merged[:half, :half] + eye, 8)
    ratio = exact(upper, corner)
    lower = merged[half:, half:] + eye - exact(merged[half:, :half], ratio)

    for copy in r_x:
        copy.wait_recv()

    def add_x(at, carry):
        part = rsum[at, x].astype(f32)
        for peer in x_at:
            part = part + rx[peer, at].astype(f32)
        r1[at] = part.astype(bf16)
        return carry

    lax.fori_loop(0, deep, add_x, 0)
    r_z = along_z(1, [(r1.at[at], rz.at[z]) for at in z_at])

    left, right = coef_in[:, :half], coef_in[:, half:]
    right = right - exact(left, ratio)
    left = exact(left, upper)
    lower = eliminate(lower, 4)
    for copy in r_z:
        copy.wait_recv()
    part = r1[z].astype(f32)
    for at in z_at:
        part = part + rz[at].astype(f32)
    part = jnp.concatenate([part, jnp.zeros_like(part)], axis=0)
    ready[...] = part.T.astype(bf16).reshape(ready.shape)
    r_y = [
        remote(ready.at[at], back_out.at[me_y], y_send.at[k], y_recv.at[k], "expert", at)
        for k, at in enumerate(y_at)
    ]
    mine = pltpu.make_async_copy(ready.at[me_y], back_out.at[me_y], y_own)
    mine.start()

    right = exact(right, eliminate(lower, 4))
    solved_out[:, half:] = right * damping
    left = left - exact(right, ratio, (((1,), (1,)), ((), ())))
    solved_out[:, :half] = left * damping

    for copy in r_y:
        copy.wait_recv()
    mine.wait()
    for copy in [gram_core, r_core, gram_last] + gram_x + r_x + gram_back + gram_z + r_z + r_y:
        copy.wait_send()


def reduce_all(r_part, gram_part, sketch, coef_t, deep, experts, hidden_total):
    rows = 256 // (CORES * WIDE)
    gram_shape = (CORES, WIDE, rows, 256)
    send_shape = (experts, 256 // experts, 128)
    return pl.pallas_call(
        functools.partial(reduce_kernel, deep, experts, hidden_total),
        out_shape=(
            jax.ShapeDtypeStruct(send_shape, bf16),
            jax.ShapeDtypeStruct((256, 256), f32),
            jax.ShapeDtypeStruct(coef_t.shape, f32),
        ),
        in_specs=[VMEM] * 4,
        out_specs=(VMEM,) * 3,
        scratch_shapes=[
            pltpu.VMEM((WIDE, rows, 256), f32),
            pltpu.VMEM((WIDE, rows, 256), f32),
            pltpu.VMEM((WIDE, rows, 256), f32),
            pltpu.VMEM((deep, rows, 256), f32),
            pltpu.VMEM(gram_shape, f32),
            pltpu.VMEM((deep, WIDE, 64, 256), bf16),
            pltpu.VMEM((deep, WIDE, 64, 256), bf16),
            pltpu.VMEM((WIDE, deep, 64, 256), bf16),
            pltpu.VMEM((deep, 64, 256), bf16),
            pltpu.VMEM((deep, 64, 256), bf16),
            pltpu.VMEM(send_shape, bf16),
            pltpu.SemaphoreType.DMA((3,)),
            pltpu.SemaphoreType.DMA((3,)),
            pltpu.SemaphoreType.DMA((4, WIDE)),
            pltpu.SemaphoreType.DMA((4, WIDE)),
            pltpu.SemaphoreType.DMA((2, deep)),
            pltpu.SemaphoreType.DMA((2, deep)),
            pltpu.SemaphoreType.DMA((experts,)),
            pltpu.SemaphoreType.DMA((experts,)),
            pltpu.SemaphoreType.DMA,
        ],
        compiler_params=pltpu.CompilerParams(
            collective_id=2, has_side_effects=True, vmem_limit_bytes=40 << 20
        ),
    )(r_part, gram_part.reshape(gram_shape), sketch, coef_t)


def per_device(tokens, cotangent, gate_logit, routes, w_up, w_down, basis, sketch):
    experts = lax.axis_size("expert")
    deep = lax.axis_size("dp") // (WIDE * CORES)
    tok_rows, width_local = tokens.shape
    capacity = min(tok_rows, tok_rows * 4 // experts)
    slot_count = experts * capacity
    gate_first = jax.nn.sigmoid(gate_logit)
    gates = jnp.stack([gate_first, 1.0 - gate_first], axis=1)
    expert_ids = jnp.arange(experts, dtype=jnp.int32)
    chosen = routes[:, :, None] == expert_ids[None, None, :]
    hit_count = jnp.sum(chosen.astype(jnp.int32), axis=1)
    gate_by_expert = jnp.sum(chosen.astype(f32) * gates[:, :, None], axis=1)
    before = jnp.cumsum(hit_count, axis=0) - hit_count
    slot_of = expert_ids[None, :] * capacity + before
    slot_ids = jnp.arange(slot_count, dtype=jnp.int32)
    slot_match = (
        (slot_of[None, :, :] == slot_ids[:, None, None]) & (hit_count[None, :, :] > 0)
    ).astype(f32)
    table = jnp.sum(slot_match, axis=2)
    gate_slot = jnp.sum(slot_match * gate_by_expert[None, :, :], axis=(1, 2))
    table_b = table.astype(bf16)
    both = jnp.concatenate([tokens, cotangent], axis=1)
    picked = jnp.dot(table_b, both, preferred_element_type=f32)
    scale = jnp.where(jnp.arange(2 * width_local)[None, :] < width_local, 1.0, gate_slot[:, None])
    packed = (picked * scale).astype(bf16).reshape(experts, capacity, 2 * width_local)
    arrived = exchange(packed, experts, 0).reshape(slot_count, 2 * width_local).T
    r_part, coef_t, gram_part = gather_compute(
        arrived[:width_local], arrived[width_local:], basis, w_up[0], w_down[0], deep
    )
    hidden_total = w_up.shape[1] * lax.axis_size("dp")
    returned, merged, solved_t = reduce_all(
        r_part, gram_part, sketch[0], coef_t, deep, experts, hidden_total
    )
    token_grad = lax.dot_general(
        table_b,
        returned.reshape(slot_count, 128)[:, :width_local],
        (((0,), (0,)), ((), ())),
        preferred_element_type=f32,
    ).astype(bf16)
    return (token_grad, merged[None], solved_t[None])


def solution(mesh):
    in_specs = (
        P("expert", "dp"),
        P("expert", "dp"),
        P("expert"),
        P("expert", None),
        P("expert", "dp", None),
        P("expert", "dp", None),
        P("dp", None),
        P("expert", None, None),
    )
    out_specs = (P("expert", "dp"), P("expert", None, None), P("expert", "dp", None))
    return jax.shard_map(
        per_device, mesh=mesh, in_specs=in_specs, out_specs=out_specs, check_vma=False
    )
```
